32 devices in a mesh: slab: 2 (over x), line: 8 (over z, y), band: 2 (over core).
Axes of the slice: x: 2, y: 2, z: 4, core: 2. Of those that a mesh axis runs over, the one named last changes fastest.
Arguments:
- cube: bfloat16 [230, 2048, 256], P('band', ('slab', 'line')), parts along dimension 1, may hold values from -6 to 6
- observed: bfloat16 [13, 2048, 256], P(None, ('slab', 'line')), parts along dimension 1, may hold values from -6 to 6
- along_kernels: bfloat16 [3, 128, 128], replicated, may hold values from -0.3125 to 0.3125
- along_offsets: int32 [3], replicated, may hold values from -1 to 1, as said below
- across_kernels: bfloat16 [3, 128, 128], replicated, may hold values from -0.3125 to 0.3125
- across_offsets: int32 [3], replicated, may hold values from -1 to 1, as said below
- resp_start: int32 [13], replicated, may hold values from 0 to 21
- resp_values: bfloat16 [13, 20], replicated, may hold values from 0.049804688 to 0.3984375
Outputs:
- synthetic: float32 [13, 2048, 256], P(None, ('slab', 'line')), parts along dimension 1
- angles: float32 [2048, 256], P(('slab', 'line')), parts along dimension 0
The draws below stay inside these ranges and needn't reach their ends.
There are 2 independent parts, one for each index of `slab`. The reference program is written for one: setup_inputs(seed, part) draws one part's arguments, and reference() takes and returns one part's arrays. A program takes and returns all parts, laid end to end along the dimension named above; an argument that names none is the same for every part. Nothing has to cross between parts.
Inputs may be any that keep to these rules, and one draw needn't show every extreme that they name: `along_offsets`: the three entries are -1, 0 and 1, each once. `across_offsets`: the three entries are -1, 0 and 1, each once.
All inputs are finite; a program needn't handle non-finite values.
Results may differ from the reference program's by a relative error of at most 0.0003.
Values may be sent and summed in bfloat16 or wider, within the bound.
A program may use at most 192 MiB of HBM per device.

```python
import jax
import jax.numpy as jnp
from jax import lax

BANDS = 230
MS = 13
BLK = 128
SPB = 10
COLS = 256
LINES = 1024
NSB = 23


def draw_along_offsets(key, part):
    return (jax.random.permutation(jax.random.fold_in(key, 11), 3) - 1).astype(jnp.int32)


def draw_across_offsets(key, part):
    return (jax.random.permutation(jax.random.fold_in(key, 23), 3) - 1).astype(jnp.int32)


def place_ends(entries, rng, low, high):
    longest = entries.shape.index(max(entries.shape))
    spots = []
    for shift in (0, 1):
        where = [jax.random.randint(jax.random.fold_in(rng, axis), (), 0, length) for axis, length in enumerate(entries.shape)]
        where[longest] = (where[longest] + shift) % entries.shape[longest]
        spots.append(tuple(where))
    return entries.at[spots[0]].set(low).at[spots[1]].set(high)


def level_of(key, dims, shards, low, high):
    factor_of = 1.0
    for dim, shards_of in shards:
        heights = jax.random.uniform(jax.random.fold_in(jax.random.fold_in(key, 6), dim), (shards_of,), jnp.float32, low / len(shards), high / len(shards))
        factor_of = factor_of * jnp.repeat(jnp.exp(heights), dims[dim] // shards_of).reshape((-1,) + (1,) * (len(dims) - 1 - dim))
    return factor_of


def bell_draw(rng, dims, scale, reach, shards=(), held_as=jnp.bfloat16):
    entries = jax.random.normal(rng, dims, jnp.float32) * scale
    if len(shards) > 0:
        entries = level_of(rng, dims, shards, -0.22, 0.18) * entries
    return jnp.clip(entries, min=-reach, max=reach).astype(held_as)


def setup_inputs(seed: int = 0, part: int = 0) -> dict:
    key_list = jax.random.split(jax.random.key(seed), 9)
    own_keys = jax.random.split(jax.random.fold_in(key_list[8], part), 9)
    cube = bell_draw(own_keys[0], (BANDS, LINES, COLS), 1.0, 6.0, ((0, 2), (1, 8)))
    observed = bell_draw(own_keys[1], (MS, LINES, COLS), 1.0, 6.0, ((1, 8),))
    along_kernels = bell_draw(key_list[2], (3, BLK, BLK), (3 * BLK) ** -0.5, 0.3125)
    along_offsets = draw_along_offsets(jax.random.fold_in(key_list[8], 71), part)
    across_kernels = bell_draw(key_list[4], (3, BLK, BLK), (3 * BLK) ** -0.5, 0.3125)
    across_offsets = draw_across_offsets(jax.random.fold_in(key_list[8], 71), part)
    resp_start = place_ends(jax.random.randint(key_list[6], (MS,), 0, NSB - 1), jax.random.fold_in(key_list[6], 1), 0, (NSB - 1) - 1).astype(jnp.int32)
    resp_values = jnp.clip(jax.random.uniform(key_list[7], (MS, 2 * SPB), jnp.float32, 0.049804688, 0.3984375), 0.049804688, 0.3984375).astype(jnp.bfloat16)
    return {"cube": cube, "observed": observed, "along_kernels": along_kernels, "along_offsets": along_offsets, "across_kernels": across_kernels, "across_offsets": across_offsets, "resp_start": resp_start, "resp_values": resp_values}


def pick_kernels(kernels, offsets):
    shifts = jnp.arange(3, dtype=jnp.int32) - 1
    onehot = (offsets[None, :] == shifts[:, None]).astype(jnp.float32)
    return jnp.einsum('sk,kpq->spq', onehot, kernels.astype(jnp.float32), precision=lax.Precision.HIGHEST)

def dense_response(resp_start, resp_values):
    bands = jnp.arange(BANDS, dtype=jnp.int32)
    local = bands[None, :] - SPB * resp_start[:, None]
    slots = jnp.arange(2 * SPB, dtype=jnp.int32)
    hits = local[:, :, None] == slots[None, None, :]
    return lax.optimization_barrier(jnp.sum(jnp.where(hits, resp_values.astype(jnp.float32)[:, None, :], jnp.float32(0.0)), axis=-1))

def along_filter(field, chosen):
    count = field.shape[1] // BLK
    blocks = field.astype(jnp.float32).reshape(field.shape[0], count, BLK, field.shape[2])
    padded = jnp.pad(blocks, ((0, 0), (1, 1), (0, 0), (0, 0)))
    total = jnp.zeros(blocks.shape, jnp.float32)
    for index in range(3):
        total = total + jnp.einsum('pq,bnqc->bnpc', chosen[index], padded[:, index:index + count], precision=lax.Precision.HIGHEST)
    return total.reshape(field.shape)

def across_filter(field, chosen):
    count = field.shape[2] // BLK
    blocks = field.astype(jnp.float32).reshape(field.shape[0], field.shape[1], count, BLK)
    padded = jnp.pad(blocks, ((0, 0), (0, 0), (1, 1), (0, 0)))
    total = jnp.zeros(blocks.shape, jnp.float32)
    for index in range(3):
        total = total + jnp.einsum('pq,blnq->blnp', chosen[index], padded[:, :, index:index + count], precision=lax.Precision.HIGHEST)
    return total.reshape(field.shape)

def reference(cube, observed, along_kernels, along_offsets, across_kernels, across_offsets, resp_start, resp_values):
    along_pick = pick_kernels(along_kernels, along_offsets)
    across_pick = pick_kernels(across_kernels, across_offsets)
    response = dense_response(resp_start, resp_values)
    groups = cube.reshape(NSB, SPB, LINES, COLS)
    weights = response.reshape(MS, NSB, SPB).transpose(1, 0, 2)

    def accumulate(carry, item):
        group, weight = item
        along = along_filter(group, along_pick)
        across = across_filter(along, across_pick)
        return (carry + jnp.einsum('mb,blc->mlc', weight, across, precision=lax.Precision.HIGHEST), None)
    start = jnp.zeros((MS, LINES, COLS), jnp.float32)
    synthetic, unused = lax.scan(accumulate, start, (groups, weights))
    seen = observed.astype(jnp.float32)
    inner = lax.optimization_barrier(jnp.sum(synthetic * seen, axis=0))
    first = jnp.sqrt(lax.optimization_barrier(jnp.sum(synthetic * synthetic, axis=0)))
    second = jnp.sqrt(lax.optimization_barrier(jnp.sum(seen * seen, axis=0)))
    angles = jnp.arccos(jnp.clip(inner / jnp.maximum(first * second, 1.0), -1.0, 1.0))
    return (synthetic, angles)
```

```python
import functools

import jax
import jax.numpy as jnp
from jax import lax
from jax.experimental import pallas as pl
from jax.experimental.pallas import tpu as pltpu
from jax.sharding import PartitionSpec as P

BLK = 128
SPB = 10
ROWS = 16
LAG = 2
MESH = pl.DeviceIdType.MESH
F32 = jnp.float32
BF16 = jnp.bfloat16


def halves(value):
    high = value.astype(BF16)
    low = (value - high.astype(F32)).astype(BF16)
    return high, low


def picked(kernels, offsets, shift):
    total = None
    for k in range(3):
        term = jnp.where(offsets[k] == shift, kernels[k].astype(F32), 0.0)
        total = term if total is None else total + term
    return total


def iota(shape, dim):
    return lax.broadcasted_iota(jnp.int32, shape, dim)


def kernel(
    sizes,
    cube,
    observed,
    along_hbm,
    across_hbm,
    values,
    along_off,
    across_off,
    start,
    synthetic,
    cosine,
    folder,
    field,
    seen,
    along,
    across,
    taps,
    mixer,
    given,
    own,
    got,
    total,
    coded,
    scale,
    near,
    near_scale,
    far,
    far_scale,
    result,
    angle_buf,
    cube_sem,
    arg_sem,
    give_sem,
    got_sem,
    send_sem,
    near_sem,
    scale_send_sem,
    near_scale_sem,
    pass_sem,
    far_sem,
    scale_pass_sem,
    far_scale_sem,
    share_sem,
    result_sem,
    out_sem,
):
    bands, lines, columns, ms, half, line_size = sizes
    groups = lines // ROWS
    core = lax.axis_index("band")
    index = lax.axis_index("line")
    other = {"band": 1 - core}
    even = index % 2 == 0
    partner = {"line": index + 1 - 2 * (index % 2)}
    step = 2 - 4 * (index % 2)
    ahead, behind = index + step, index - step
    has_ahead = jnp.logical_and(ahead >= 0, ahead < line_size)
    has_behind = jnp.logical_and(behind >= 0, behind < line_size)

    def cube_copy(g):
        return pltpu.make_async_copy(
            cube.at[:, pl.ds(g * ROWS, ROWS), :], field.at[g], cube_sem.at[g]
        )

    along_copy = pltpu.make_async_copy(along_hbm, along, arg_sem.at[0])
    across_copy = pltpu.make_async_copy(across_hbm, across, arg_sem.at[1])
    seen_copy = pltpu.make_async_copy(observed, seen, arg_sem.at[2])
    for g in range(groups):
        cube_copy(g).start()
    along_copy.start()
    across_copy.start()
    seen_copy.start()

    barrier = pltpu.get_barrier_semaphore()
    pl.semaphore_signal(barrier, inc=1, device_id=other, device_id_type=MESH)
    pl.semaphore_signal(barrier, inc=1, device_id=partner, device_id_type=MESH)

    @pl.when(has_ahead)
    def _():
        pl.semaphore_signal(barrier, inc=1, device_id={"line": ahead}, device_id_type=MESH)

    @pl.when(has_behind)
    def _():
        pl.semaphore_signal(barrier, inc=1, device_id={"line": behind}, device_id_type=MESH)

    lane = core * bands + iota((ms, 128), 1)
    row = iota((ms, 128), 0)
    first = jnp.zeros((ms, 128), jnp.int32)
    for m in range(ms):
        first = jnp.where(row == m, start[m], first)
    slot = lane - SPB * first
    weights = values[...].astype(F32)
    response = jnp.zeros((ms, 128), F32)
    for j in range(2 * SPB):
        response = jnp.where(slot == j, weights[:, j : j + 1], response)
    tall = 2 * half * ROWS
    picks = iota((tall, ms), 0) // ROWS
    owner = jnp.where(picks < half, (1 - core) * half + picks, core * half + picks - half)
    choose = (owner == iota((tall, ms), 1)).astype(BF16)
    per_row = jnp.dot(choose, response.astype(BF16), preferred_element_type=F32).astype(BF16)
    wide = bands * ROWS
    spread = (iota((128, wide), 1) // ROWS == iota((128, wide), 0)).astype(BF16)
    spread_rows = jnp.dot(per_row, spread, preferred_element_type=F32)
    same = iota((tall, wide), 0) % ROWS == iota((tall, wide), 1) % ROWS
    folder[...] = jnp.where(same, spread_rows, 0.0).astype(BF16)

    peers = 2 + has_ahead.astype(jnp.int32) + has_behind.astype(jnp.int32)
    pl.semaphore_wait(barrier, peers)

    def give_copy(g):
        return pltpu.make_async_remote_copy(
            src_ref=given.at[g],
            dst_ref=got.at[g],
            send_sem=give_sem.at[g],
            recv_sem=got_sem.at[g],
            device_id=other,
            device_id_type=MESH,
        )

    def fold(g, carry):
        cube_copy(g).wait()
        block = field[g].reshape(wide, columns)
        part = jnp.dot(folder[...], block, preferred_element_type=F32)
        part = part.reshape(2 * half, ROWS, columns)
        given[g] = part[:half]
        own[g] = part[half:]
        give_copy(g).start()
        return carry

    lax.fori_loop(0, groups, fold, 0)

    along_copy.wait()
    across_copy.wait()
    before, after = (picked(along, along_off, -1), picked(along, along_off, 1))
    middle = picked(along, along_off, 0)
    near_tap = jnp.where(even, after, before)
    far_tap = jnp.where(even, before, after)
    for slot_index, tap in enumerate((middle, near_tap, far_tap)):
        tap = tap.astype(BF16)
        taps[slot_index] = jnp.concatenate([tap, tap], axis=1)
    count = columns // BLK
    mixer[...] = jnp.zeros(mixer.shape, BF16)
    for shift in (-1, 0, 1):
        turned = jnp.transpose(picked(across, across_off, shift)).astype(BF16)
        for j in range(count):
            if 0 <= j + shift < count:
                for part in range(2):
                    top = part * columns + (j + shift) * BLK
                    mixer[top : top + BLK, j * BLK : (j + 1) * BLK] = turned

    def code_copies(m):
        return (
            pltpu.make_async_remote_copy(
                src_ref=coded.at[m],
                dst_ref=near.at[m],
                send_sem=send_sem.at[m],
                recv_sem=near_sem.at[m],
                device_id=partner,
                device_id_type=MESH,
            ),
            pltpu.make_async_remote_copy(
                src_ref=scale.at[m],
                dst_ref=near_scale.at[m],
                send_sem=scale_send_sem.at[m],
                recv_sem=near_scale_sem.at[m],
                device_id=partner,
                device_id_type=MESH,
            ),
        )

    def pass_copies(m):
        return (
            pltpu.make_async_remote_copy(
                src_ref=near.at[m],
                dst_ref=far.at[m],
                send_sem=pass_sem.at[m],
                recv_sem=far_sem.at[m],
                device_id={"line": ahead},
                device_id_type=MESH,
            ),
            pltpu.make_async_remote_copy(
                src_ref=near_scale.at[m],
                dst_ref=far_scale.at[m],
                send_sem=scale_pass_sem.at[m],
                recv_sem=far_scale_sem.at[m],
                device_id={"line": ahead},
                device_id_type=MESH,
            ),
        )

    def share_copy(m):
        return pltpu.make_async_remote_copy(
            src_ref=result.at[0, m],
            dst_ref=result.at[1, m],
            send_sem=share_sem.at[m],
            recv_sem=result_sem.at[m],
            device_id=other,
            device_id_type=MESH,
        )

    def out_copy(which, m):
        place = core if which == 0 else 1 - core
        return pltpu.make_async_copy(
            result.at[which, m], synthetic.at[place * half + m], out_sem.at[which, m]
        )

    def guard(m, place, body):
        if half + m < ms:
            body()
        else:
            pl.when(place * half + m < ms)(body)

    @pl.when(jnp.logical_not(has_behind))
    def _():
        far[...] = jnp.zeros(far.shape, jnp.int16)
        far_scale[...] = jnp.zeros(far_scale.shape, F32)

    for g in range(groups):
        give_copy(g).wait_recv()

    for m in range(half):

        def encode(m=m):
            value = (own[:, m] + got[:, m]).reshape(lines, columns)
            total[m] = value
            peak = jnp.max(jnp.abs(value), axis=0, keepdims=True)
            inverse = jnp.where(peak > 0.0, 32767.0 / jnp.maximum(peak, 1e-30), 0.0)
            coded[m] = jnp.round(value * inverse).astype(jnp.int32).astype(jnp.int16)
            scale[m] = peak * (1.0 / 32767.0)
            for copy in code_copies(m):
                copy.start()

        guard(m, core, encode)

    seen_copy.wait()

    def filtered(slot_index, value):
        high, low = halves(value)
        stacked = jnp.concatenate([high, low], axis=0)
        return jnp.dot(taps[slot_index], stacked, preferred_element_type=F32)

    def arrive(m):
        copies = code_copies(m)
        for copy in copies:
            copy.wait_recv()

        @pl.when(has_ahead)
        def _():
            for copy in pass_copies(m):
                copy.start()

        total[m] = (
            filtered(0, total[m])
            + filtered(1, near[m].astype(jnp.int32).astype(F32)) * near_scale[m]
        )

    def finish(m):
        @pl.when(has_behind)
        def _():
            for copy in pass_copies(m):
                copy.wait_recv()

        smooth = total[m] + filtered(2, far[m].astype(jnp.int32).astype(F32)) * far_scale[m]
        high, low = halves(smooth)
        both = jnp.concatenate([high, low], axis=1)
        result[0, m] = jnp.dot(both, mixer[...], preferred_element_type=F32)
        share_copy(m).start()
        out_copy(0, m).start()

    for tick in range(half + LAG):
        if tick < half:
            guard(tick, core, functools.partial(arrive, tick))
        if tick >= LAG:
            guard(tick - LAG, core, functools.partial(finish, tick - LAG))

    for m in range(half):

        def receive(m=m):
            share_copy(m).wait_recv()
            out_copy(1, m).start()

        guard(m, 1 - core, receive)

    def angle(r, carry):
        rows = pl.ds(r * ROWS, ROWS)
        inner = power = level = None
        for which in range(2):
            place = core if which == 0 else 1 - core
            sums = [jnp.zeros((ROWS, columns), F32)] * 3
            for m in range(half):
                spot = place * half + m
                valid = spot < ms
                look = jnp.minimum(spot, ms - 1)
                mine = result[which, m, rows, :]
                sight = seen[look, rows, :].astype(F32)
                if half + m >= ms:
                    mine = jnp.where(valid, mine, 0.0)
                    sight = jnp.where(valid, sight, 0.0)
                sums = [
                    sums[0] + mine * sight,
                    sums[1] + mine * mine,
                    sums[2] + sight * sight,
                ]
            inner = sums[0] if inner is None else inner + sums[0]
            power = sums[1] if power is None else power + sums[1]
            level = sums[2] if level is None else level + sums[2]
        norm = jnp.maximum(jnp.sqrt(power) * jnp.sqrt(level), 1.0)
        angle_buf[rows, :] = jnp.clip(inner / norm, -1.0, 1.0)
        return carry

    def blank(which, place):
        for m in range(half):
            if half + m >= ms:

                @pl.when(place * half + m >= ms)
                def _():
                    result[which, m] = jnp.zeros((lines, columns), F32)

    blank(0, core)
    blank(1, 1 - core)
    lax.fori_loop(0, lines // ROWS, angle, 0)
    cos_copy = pltpu.make_async_copy(angle_buf, cosine, arg_sem.at[3])
    cos_copy.start()

    for g in range(groups):
        give_copy(g).wait_send()
    for m in range(half):

        def drain(m=m):
            for copy in code_copies(m):
                copy.wait_send()

            @pl.when(has_ahead)
            def _():
                for copy in pass_copies(m):
                    copy.wait_send()

            share_copy(m).wait_send()
            out_copy(0, m).wait()

        guard(m, core, drain)
        guard(m, 1 - core, lambda m=m: out_copy(1, m).wait())
    cos_copy.wait()


def on_device(
    cube,
    observed,
    along_kernels,
    along_offsets,
    across_kernels,
    across_offsets,
    resp_start,
    resp_values,
):
    bands, lines, columns = cube.shape
    ms = observed.shape[0]
    cores = lax.axis_size("band")
    line_size = lax.axis_size("line")
    assert cores == 2 and line_size % 2 == 0 and lines == BLK and bands <= 128
    half = -(-ms // cores)
    groups = lines // ROWS
    sizes = (bands, lines, columns, ms, half, line_size)
    hbm = pl.BlockSpec(memory_space=pltpu.HBM)
    vmem = pl.BlockSpec(memory_space=pltpu.VMEM)
    smem = pl.BlockSpec(memory_space=pltpu.SMEM)
    dma = pltpu.SemaphoreType.DMA
    synthetic, cosine = pl.pallas_call(
        functools.partial(kernel, sizes),
        out_shape=(
            jax.ShapeDtypeStruct((ms, lines, columns), F32),
            jax.ShapeDtypeStruct((lines, columns), F32),
        ),
        in_specs=[hbm, hbm, hbm, hbm, vmem, smem, smem, smem],
        out_specs=(hbm, hbm),
        scratch_shapes=[
            pltpu.VMEM((2 * half * ROWS, bands * ROWS), BF16),
            pltpu.VMEM((groups, bands, ROWS, columns), BF16),
            pltpu.VMEM((ms, lines, columns), BF16),
            pltpu.VMEM((3, BLK, BLK), BF16),
            pltpu.VMEM((3, BLK, BLK), BF16),
            pltpu.VMEM((3, BLK, 2 * BLK), BF16),
            pltpu.VMEM((2 * columns, columns), BF16),
            pltpu.VMEM((groups, half, ROWS, columns), F32),
            pltpu.VMEM((groups, half, ROWS, columns), F32),
            pltpu.VMEM((groups, half, ROWS, columns), F32),
            pltpu.VMEM((half, lines, columns), F32),
            pltpu.VMEM((half, lines, columns), jnp.int16),
            pltpu.VMEM((half, 1, columns), F32),
            pltpu.VMEM((half, lines, columns), jnp.int16),
            pltpu.VMEM((half, 1, columns), F32),
            pltpu.VMEM((half, lines, columns), jnp.int16),
            pltpu.VMEM((half, 1, columns), F32),
            pltpu.VMEM((2, half, lines, columns), F32),
            pltpu.VMEM((lines, columns), F32),
            dma((groups,)),
            dma((4,)),
            dma((groups,)),
            dma((groups,)),
        ]
        + [dma((half,))] * 10
        + [dma((2, half))],
        compiler_params=pltpu.CompilerParams(
            collective_id=0, has_side_effects=True, vmem_limit_bytes=48 * 2**20
        ),
    )(
        cube,
        observed,
        along_kernels,
        across_kernels,
        resp_values,
        along_offsets,
        across_offsets,
        resp_start,
    )
    return synthetic, jnp.arccos(cosine)


def solution(mesh):
    placed = (
        P("band", ("slab", "line"), None),
        P(None, ("slab", "line"), None),
        P(),
        P(),
        P(),
        P(),
        P(),
        P(),
    )
    return jax.shard_map(
        on_device,
        mesh=mesh,
        in_specs=placed,
        out_specs=(P(None, ("slab", "line"), None), P(("slab", "line"), None)),
        check_vma=False,
    )
```

```python
import functools

import jax
import jax.numpy as jnp
from jax import lax
from jax.experimental import pallas as pl
from jax.experimental.pallas import tpu as pltpu
from jax.sharding import PartitionSpec as P

BLK = 128
SPB = 10
ROWS = 16
LAG = 2
MESH = pl.DeviceIdType.MESH
F32 = jnp.float32
BF16 = jnp.bfloat16


def halves(value):
    high = value.astype(BF16)
    low = (value - high.astype(F32)).astype(BF16)
    return high, low


def picked(kernels, offsets, shift):
    total = None
    for k in range(3):
        term = jnp.where(offsets[k] == shift, kernels[k].astype(F32), 0.0)
        total = term if total is None else total + term
    return total


def iota(shape, dim):
    return lax.broadcasted_iota(jnp.int32, shape, dim)


def kernel(
    sizes,
    cube,
    observed,
    along_hbm,
    across_hbm,
    values_hbm,
    along_off_hbm,
    across_off_hbm,
    start_hbm,
    synthetic,
    cosine,
    folder,
    field,
    seen,
    along,
    across,
    taps,
    mixer,
    given,
    own,
    got,
    total,
    coded,
    scale,
    near,
    near_scale,
    far,
    far_scale,
    result,
    angle_buf,
    values,
    along_off,
    across_off,
    start,
    cube_sem,
    arg_sem,
    give_sem,
    got_sem,
    send_sem,
    near_sem,
    scale_send_sem,
    near_scale_sem,
    pass_sem,
    far_sem,
    scale_pass_sem,
    far_scale_sem,
    share_sem,
    result_sem,
    out_sem,
):
    bands, lines, columns, ms, half, line_size = sizes
    groups = lines // ROWS
    core = lax.axis_index("band")
    index = lax.axis_index("line")
    other = {"band": 1 - core}
    even = index % 2 == 0
    partner = {"line": index + 1 - 2 * (index % 2)}
    step = 2 - 4 * (index % 2)
    ahead, behind = index + step, index - step
    has_ahead = jnp.logical_and(ahead >= 0, ahead < line_size)
    has_behind = jnp.logical_and(behind >= 0, behind < line_size)

    def cube_copy(g):
        return pltpu.make_async_copy(
            cube.at[:, pl.ds(g * ROWS, ROWS), :], field.at[g], cube_sem.at[g]
        )

    along_copy = pltpu.make_async_copy(along_hbm, along, arg_sem.at[0])
    across_copy = pltpu.make_async_copy(across_hbm, across, arg_sem.at[1])
    seen_copy = pltpu.make_async_copy(observed, seen, arg_sem.at[2])
    early = [
        pltpu.make_async_copy(values_hbm, values, arg_sem.at[4]),
        pltpu.make_async_copy(start_hbm, start, arg_sem.at[5]),
        pltpu.make_async_copy(along_off_hbm, along_off, arg_sem.at[6]),
        pltpu.make_async_copy(across_off_hbm, across_off, arg_sem.at[7]),
    ]
    for copy in early:
        copy.start()
    for g in range(groups):
        cube_copy(g).start()
    along_copy.start()
    across_copy.start()
    seen_copy.start()

    barrier = pltpu.get_barrier_semaphore()
    pl.semaphore_signal(barrier, inc=1, device_id=other, device_id_type=MESH)
    pl.semaphore_signal(barrier, inc=1, device_id=partner, device_id_type=MESH)

    @pl.when(has_ahead)
    def _():
        pl.semaphore_signal(barrier, inc=1, device_id={"line": ahead}, device_id_type=MESH)

    @pl.when(has_behind)
    def _():
        pl.semaphore_signal(barrier, inc=1, device_id={"line": behind}, device_id_type=MESH)

    for copy in early:
        copy.wait()

    lane = core * bands + iota((ms, 128), 1)
    row = iota((ms, 128), 0)
    first = jnp.zeros((ms, 128), jnp.int32)
    for m in range(ms):
        first = jnp.where(row == m, start[m], first)
    slot = lane - SPB * first
    weights = values[...].astype(F32)
    response = jnp.zeros((ms, 128), F32)
    for j in range(2 * SPB):
        response = jnp.where(slot == j, weights[:, j : j + 1], response)
    tall = 2 * half * ROWS
    picks = iota((tall, ms), 0) // ROWS
    owner = jnp.where(picks < half, (1 - core) * half + picks, core * half + picks - half)
    choose = (owner == iota((tall, ms), 1)).astype(BF16)
    per_row = jnp.dot(choose, response.astype(BF16), preferred_element_type=F32).astype(BF16)
    wide = bands * ROWS
    spread = (iota((128, wide), 1) // ROWS == iota((128, wide), 0)).astype(BF16)
    spread_rows = jnp.dot(per_row, spread, preferred_element_type=F32)
    same = iota((tall, wide), 0) % ROWS == iota((tall, wide), 1) % ROWS
    folder[...] = jnp.where(same, spread_rows, 0.0).astype(BF16)

    peers = 2 + has_ahead.astype(jnp.int32) + has_behind.astype(jnp.int32)
    pl.semaphore_wait(barrier, peers)

    def give_copy(g):
        return pltpu.make_async_remote_copy(
            src_ref=given.at[g],
            dst_ref=got.at[g],
            send_sem=give_sem.at[g],
            recv_sem=got_sem.at[g],
            device_id=other,
            device_id_type=MESH,
        )

    def fold(g, carry):
        cube_copy(g).wait()
        block = field[g].reshape(wide, columns)
        part = jnp.dot(folder[...], block, preferred_element_type=F32)
        part = part.reshape(2 * half, ROWS, columns)
        given[g] = part[:half]
        own[g] = part[half:]
        give_copy(g).start()
        return carry

    lax.fori_loop(0, groups, fold, 0)

    along_copy.wait()
    across_copy.wait()
    before, after = (picked(along, along_off, -1), picked(along, along_off, 1))
    middle = picked(along, along_off, 0)
    near_tap = jnp.where(even, after, before)
    far_tap = jnp.where(even, before, after)
    for slot_index, tap in enumerate((middle, near_tap, far_tap)):
        tap = tap.astype(BF16)
        taps[slot_index] = jnp.concatenate([tap, tap], axis=1)
    count = columns // BLK
    mixer[...] = jnp.zeros(mixer.shape, BF16)
    for shift in (-1, 0, 1):
        turned = jnp.transpose(picked(across, across_off, shift)).astype(BF16)
        for j in range(count):
            if 0 <= j + shift < count:
                for part in range(2):
                    top = part * columns + (j + shift) * BLK
                    mixer[top : top + BLK, j * BLK : (j + 1) * BLK] = turned

    def code_copies(m):
        return (
            pltpu.make_async_remote_copy(
                src_ref=coded.at[m],
                dst_ref=near.at[m],
                send_sem=send_sem.at[m],
                recv_sem=near_sem.at[m],
                device_id=partner,
                device_id_type=MESH,
            ),
            pltpu.make_async_remote_copy(
                src_ref=scale.at[m],
                dst_ref=near_scale.at[m],
                send_sem=scale_send_sem.at[m],
                recv_sem=near_scale_sem.at[m],
                device_id=partner,
                device_id_type=MESH,
            ),
        )

    def pass_copies(m):
        return (
            pltpu.make_async_remote_copy(
                src_ref=near.at[m],
                dst_ref=far.at[m],
                send_sem=pass_sem.at[m],
                recv_sem=far_sem.at[m],
                device_id={"line": ahead},
                device_id_type=MESH,
            ),
            pltpu.make_async_remote_copy(
                src_ref=near_scale.at[m],
                dst_ref=far_scale.at[m],
                send_sem=scale_pass_sem.at[m],
                recv_sem=far_scale_sem.at[m],
                device_id={"line": ahead},
                device_id_type=MESH,
            ),
        )

    def share_copy(m):
        return pltpu.make_async_remote_copy(
            src_ref=result.at[0, m],
            dst_ref=result.at[1, m],
            send_sem=share_sem.at[m],
            recv_sem=result_sem.at[m],
            device_id=other,
            device_id_type=MESH,
        )

    def out_copy(which, m):
        place = core if which == 0 else 1 - core
        return pltpu.make_async_copy(
            result.at[which, m], synthetic.at[place * half + m], out_sem.at[which, m]
        )

    def guard(m, place, body):
        if half + m < ms:
            body()
        else:
            pl.when(place * half + m < ms)(body)

    @pl.when(jnp.logical_not(has_behind))
    def _():
        far[...] = jnp.zeros(far.shape, jnp.int16)
        far_scale[...] = jnp.zeros(far_scale.shape, F32)

    for g in range(groups):
        give_copy(g).wait_recv()

    for m in range(half):

        def encode(m=m):
            value = (own[:, m] + got[:, m]).reshape(lines, columns)
            total[m] = value
            peak = jnp.max(jnp.abs(value), axis=0, keepdims=True)
            inverse = jnp.where(peak > 0.0, 32767.0 / jnp.maximum(peak, 1e-30), 0.0)
            coded[m] = jnp.round(value * inverse).astype(jnp.int32).astype(jnp.int16)
            scale[m] = peak * (1.0 / 32767.0)
            for copy in code_copies(m):
                copy.start()

        guard(m, core, encode)

    seen_copy.wait()

    def filtered(slot_index, value):
        high, low = halves(value)
        stacked = jnp.concatenate([high, low], axis=0)
        return jnp.dot(taps[slot_index], stacked, preferred_element_type=F32)

    def arrive(m):
        copies = code_copies(m)
        for copy in copies:
            copy.wait_recv()

        @pl.when(has_ahead)
        def _():
            for copy in pass_copies(m):
                copy.start()

        total[m] = (
            filtered(0, total[m])
            + filtered(1, near[m].astype(jnp.int32).astype(F32)) * near_scale[m]
        )

    def finish(m):
        @pl.when(has_behind)
        def _():
            for copy in pass_copies(m):
                copy.wait_recv()

        smooth = total[m] + filtered(2, far[m].astype(jnp.int32).astype(F32)) * far_scale[m]
        high, low = halves(smooth)
        both = jnp.concatenate([high, low], axis=1)
        result[0, m] = jnp.dot(both, mixer[...], preferred_element_type=F32)
        share_copy(m).start()
        out_copy(0, m).start()

    for tick in range(half + LAG):
        if tick < half:
            guard(tick, core, functools.partial(arrive, tick))
        if tick >= LAG:
            guard(tick - LAG, core, functools.partial(finish, tick - LAG))

    for m in range(half):

        def receive(m=m):
            share_copy(m).wait_recv()
            out_copy(1, m).start()

        guard(m, 1 - core, receive)

    def angle(r, carry):
        rows = pl.ds(r * ROWS, ROWS)
        inner = power = level = None
        for which in range(2):
            place = core if which == 0 else 1 - core
            sums = [jnp.zeros((ROWS, columns), F32)] * 3
            for m in range(half):
                spot = place * half + m
                valid = spot < ms
                look = jnp.minimum(spot, ms - 1)
                mine = result[which, m, rows, :]
                sight = seen[look, rows, :].astype(F32)
                if half + m >= ms:
                    mine = jnp.where(valid, mine, 0.0)
                    sight = jnp.where(valid, sight, 0.0)
                sums = [
                    sums[0] + mine * sight,
                    sums[1] + mine * mine,
                    sums[2] + sight * sight,
                ]
            inner = sums[0] if inner is None else inner + sums[0]
            power = sums[1] if power is None else power + sums[1]
            level = sums[2] if level is None else level + sums[2]
        norm = jnp.maximum(jnp.sqrt(power) * jnp.sqrt(level), 1.0)
        angle_buf[rows, :] = jnp.clip(inner / norm, -1.0, 1.0)
        return carry

    def blank(which, place):
        for m in range(half):
            if half + m >= ms:

                @pl.when(place * half + m >= ms)
                def _():
                    result[which, m] = jnp.zeros((lines, columns), F32)

    blank(0, core)
    blank(1, 1 - core)
    lax.fori_loop(0, lines // ROWS, angle, 0)
    cos_copy = pltpu.make_async_copy(angle_buf, cosine, arg_sem.at[3])
    cos_copy.start()

    for g in range(groups):
        give_copy(g).wait_send()
    for m in range(half):

        def drain(m=m):
            for copy in code_copies(m):
                copy.wait_send()

            @pl.when(has_ahead)
            def _():
                for copy in pass_copies(m):
                    copy.wait_send()

            share_copy(m).wait_send()
            out_copy(0, m).wait()

        guard(m, core, drain)
        guard(m, 1 - core, lambda m=m: out_copy(1, m).wait())
    cos_copy.wait()


def on_device(
    cube,
    observed,
    along_kernels,
    along_offsets,
    across_kernels,
    across_offsets,
    resp_start,
    resp_values,
):
    bands, lines, columns = cube.shape
    ms = observed.shape[0]
    cores = lax.axis_size("band")
    line_size = lax.axis_size("line")
    assert cores == 2 and line_size % 2 == 0 and lines == BLK and bands <= 128
    half = -(-ms // cores)
    groups = lines // ROWS
    sizes = (bands, lines, columns, ms, half, line_size)
    hbm = pl.BlockSpec(memory_space=pltpu.HBM)
    dma = pltpu.SemaphoreType.DMA
    synthetic, cosine = pl.pallas_call(
        functools.partial(kernel, sizes),
        out_shape=(
            jax.ShapeDtypeStruct((ms, lines, columns), F32),
            jax.ShapeDtypeStruct((lines, columns), F32),
        ),
        in_specs=[hbm] * 8,
        out_specs=(hbm, hbm),
        scratch_shapes=[
            pltpu.VMEM((2 * half * ROWS, bands * ROWS), BF16),
            pltpu.VMEM((groups, bands, ROWS, columns), BF16),
            pltpu.VMEM((ms, lines, columns), BF16),
            pltpu.VMEM((3, BLK, BLK), BF16),
            pltpu.VMEM((3, BLK, BLK), BF16),
            pltpu.VMEM((3, BLK, 2 * BLK), BF16),
            pltpu.VMEM((2 * columns, columns), BF16),
            pltpu.VMEM((groups, half, ROWS, columns), F32),
            pltpu.VMEM((groups, half, ROWS, columns), F32),
            pltpu.VMEM((groups, half, ROWS, columns), F32),
            pltpu.VMEM((half, lines, columns), F32),
            pltpu.VMEM((half, lines, columns), jnp.int16),
            pltpu.VMEM((half, 1, columns), F32),
            pltpu.VMEM((half, lines, columns), jnp.int16),
            pltpu.VMEM((half, 1, columns), F32),
            pltpu.VMEM((half, lines, columns), jnp.int16),
            pltpu.VMEM((half, 1, columns), F32),
            pltpu.VMEM((2, half, lines, columns), F32),
            pltpu.VMEM((lines, columns), F32),
            pltpu.VMEM(resp_values.shape, BF16),
            pltpu.SMEM(along_offsets.shape, jnp.int32),
            pltpu.SMEM(across_offsets.shape, jnp.int32),
            pltpu.SMEM(resp_start.shape, jnp.int32),
            dma((groups,)),
            dma((8,)),
            dma((groups,)),
            dma((groups,)),
        ]
        + [dma((half,))] * 10
        + [dma((2, half))],
        compiler_params=pltpu.CompilerParams(
            collective_id=0, has_side_effects=True, vmem_limit_bytes=67_043_328
        ),
    )(
        cube,
        observed,
        along_kernels,
        across_kernels,
        resp_values,
        along_offsets,
        across_offsets,
        resp_start,
    )
    return synthetic, jnp.arccos(cosine)


def solution(mesh):
    placed = (
        P("band", ("slab", "line"), None),
        P(None, ("slab", "line"), None),
        P(),
        P(),
        P(),
        P(),
        P(),
        P(),
    )
    return jax.shard_map(
        on_device,
        mesh=mesh,
        in_specs=placed,
        out_specs=(P(None, ("slab", "line"), None), P(("slab", "line"), None)),
        check_vma=False,
    )
```
